256 devices in a mesh: row: 16 (over z, y_hi), col: 16 (over y_lo, x, core).
Axes of the slice: x: 4, y: 4 (y_hi: 2, y_lo: 2; y = y_hi * 2 + y_lo), z: 8, core: 2. Of those that a mesh axis runs over, the one named last changes fastest.
Arguments:
- diag_block: float32 [2048, 2048], P('row'), as said below
- z_panel: float32 [2048, 2048], P('row', 'col'), may hold values from -0.046875 to 0.046875
- panel_below: float32 [32768, 2048], P('row', 'col'), may hold values from -6 to 6
- z_trail: float32 [32768, 2048], P('row', 'col'), may hold values from -6 to 6
- norm_sq: float32 [2048], P('col'), may hold values from 0.05 to 0.5
Outputs:
- norm_out: float32 [2048], P('col')
- trail_out: float32 [32768, 2048], P('row', 'col')
The draws below stay inside these ranges and needn't reach their ends.
Inputs may be any that keep to these rules, and one draw needn't show every extreme that they name: diag_block is zero above its diagonal; its diagonal entries are at least 1.
All inputs are finite; a program needn't handle non-finite values.
Results may differ from the reference program's by a relative error of at most 0.00017.
Values sent between devices are 32-bit elements; how exact they have to be, the bound alone decides.
A program may use at most 64 MiB of HBM per device.

```python
import math
import jax
import jax.numpy as jnp
from jax import lax

NB = 2048
OBS = 2048
TRAIL = 32768


def draw_diag_block(key, part):
    key_lower, key_pivot = jax.random.split(jax.random.fold_in(key, 11))
    rows = lax.broadcasted_iota(jnp.int32, (NB, NB), 0)
    cols = lax.broadcasted_iota(jnp.int32, (NB, NB), 1)
    lower = jax.random.normal(key_lower, (NB, NB), jnp.float32) * (4.0 / math.sqrt(NB))
    pivots = jax.random.uniform(key_pivot, (NB, NB), jnp.float32, 1.0, 2.0)
    return jnp.where(rows > cols, lower, jnp.where(rows == cols, pivots, 0.0)).astype(jnp.float32)


def shard_levels(stream_key, extent, cuts, smallest, high):
    loudness = 1.0
    for position, blocks in cuts:
        draws = jax.random.uniform(jax.random.fold_in(jax.random.fold_in(stream_key, 6), position), (blocks,), jnp.float32, smallest / len(cuts), high / len(cuts))
        loudness = loudness * jnp.repeat(jnp.exp(draws), extent[position] // blocks).reshape((-1,) + (1,) * (len(extent) - 1 - position))
    return loudness


def bell_draw(key, extent, width, most, cuts=(), kind=jnp.bfloat16):
    gain = shard_levels(key, extent, cuts, -0.22, 0.18) if cuts else 1.0
    result = jax.random.normal(key, extent, jnp.float32) * width * gain
    return jnp.minimum(jnp.maximum(result, -most), most).astype(kind)


def setup_inputs(seed: int = 0) -> dict:
    arg_keys = jax.random.split(jax.random.key(seed), 6)
    diag_block = draw_diag_block(jax.random.fold_in(arg_keys[5], 71), 0)
    z_panel = bell_draw(arg_keys[1], (NB, OBS), (8 * NB) ** -0.5, 0.046875, ((0, 16), (1, 16)), jnp.float32)
    panel_below = bell_draw(arg_keys[2], (TRAIL, NB), 1.0, 6.0, ((0, 16), (1, 16)), jnp.float32)
    z_trail = bell_draw(arg_keys[3], (TRAIL, OBS), 1.0, 6.0, ((0, 16), (1, 16)), jnp.float32)
    norm_sq = jnp.clip(0.05 + 0.45 * jax.random.uniform(arg_keys[4], (OBS,), jnp.float32) ** shard_levels(arg_keys[4], (OBS,), ((0, 16),), -0.2, 0.2), 0.05, 0.5)
    return {"diag_block": diag_block, "z_panel": z_panel, "panel_below": panel_below, "z_trail": z_trail, "norm_sq": norm_sq}


def reference(diag_block, z_panel, panel_below, z_trail, norm_sq):
    solved = lax.linalg.triangular_solve(diag_block, z_panel, left_side=True, lower=True)
    norm_out = norm_sq + jnp.sum(solved * solved, axis=0)
    update = jnp.dot(panel_below.astype(jnp.float32), solved.astype(jnp.float32), precision=lax.Precision.HIGHEST, preferred_element_type=jnp.float32)
    trail_out = z_trail - update
    return (norm_out, trail_out)
```

```python
import jax
import jax.numpy as jnp
from jax import lax
from jax.experimental import pallas as pl
from jax.experimental.pallas import tpu as pltpu
from jax.sharding import PartitionSpec as P

F32 = jnp.float32
BF16 = jnp.bfloat16
T = 128
PIECES = 4


def halves(v):
    high = v.astype(BF16)
    low = (v - high.astype(F32)).astype(BF16)
    return high, low


def left_form(v):
    high, low = halves(v)
    return jnp.concatenate([high, low], axis=1)


def right_form(v):
    high, low = halves(v)
    both = jnp.concatenate([high, low], axis=1)
    return jnp.concatenate([both, both], axis=0)


def product(left, right):
    wide = jnp.dot(left, right, preferred_element_type=F32)
    return wide[:, :T] + wide[:, T:]


def invert_lower(blocks):
    rows = lax.broadcasted_iota(jnp.int32, (T, T), 0)
    cols = lax.broadcasted_iota(jnp.int32, (T, T), 1)
    on_diag = rows == cols
    found = [jnp.where(on_diag, 1.0 / jnp.where(on_diag, b, 1.0), 0.0) for b in blocks]
    size = 1
    while size < T:
        below = (
            (rows // (2 * size) == cols // (2 * size))
            & ((rows // size) % 2 == 1)
            & ((cols // size) % 2 == 0)
        )
        offs = [jnp.where(below, b, 0.0) for b in blocks]
        mids = [product(left_form(o), right_form(x)) for o, x in zip(offs, found)]
        found = [x - product(left_form(x), right_form(m)) for x, m in zip(found, mids)]
        size *= 2
    return found


def kernel(
    d_hbm, z_hbm, a_hbm, norm_ref,
    norm_out, update_ref,
    panel, lower, zbuf, acc, solved, solved_right, inverse,
    own_sem, send_a, recv_a, send_l, recv_l, send_z, recv_z, send_s, recv_s,
):
    row = lax.axis_index("row")
    col = lax.axis_index("col")
    z, hi = row // 2, row % 2
    lo, x, core = col // 8, (col // 2) % 4, col % 2
    height = a_hbm.shape[0]
    piece_rows = height // PIECES
    planes = 8

    def place(lo_, x_, core_):
        return lo_ * 8 + x_ * 2 + core_

    x_next, x_prev, x_far = (x + 1) % 4, (x + 3) % 4, (x + 2) % 4
    to_x_next = {"row": row, "col": place(lo, x_next, core)}
    to_x_prev = {"row": row, "col": place(lo, x_prev, core)}
    to_y = {"row": row, "col": place(1 - lo, x, core)}
    to_sibling = {"row": row, "col": place(lo, x, 1 - core)}
    to_pair_l = {"row": z * 2 + 1 - hi, "col": place(1 - lo, x, core)}
    to_pair_z = {"row": z * 2 + 1 - hi, "col": col}
    to_z_next = {"row": ((z + 1) % planes) * 2 + hi, "col": col}
    to_z_prev = {"row": ((z + planes - 1) % planes) * 2 + hi, "col": col}
    partners = [to_x_next, to_x_prev, to_y, to_sibling, to_pair_l, to_pair_z, to_z_next, to_z_prev]

    own_copies = [pltpu.make_async_copy(a_hbm, panel.at[col], own_sem.at[0])]
    own_copies.append(pltpu.make_async_copy(z_hbm, zbuf.at[hi], own_sem.at[1]))
    for j in range(planes):
        own_copies.append(
            pltpu.make_async_copy(d_hbm.at[:, pl.ds(2 * T * j, 2 * T)], lower.at[hi, j], own_sem.at[2 + j])
        )
    for c in own_copies:
        c.start()

    barrier = pltpu.get_barrier_semaphore()
    for d in partners:
        pl.semaphore_signal(barrier, inc=1, device_id=d, device_id_type=pl.DeviceIdType.MESH)
    pl.semaphore_wait(barrier, len(partners))

    def remote(src, dst, s, r, target):
        return pltpu.make_async_remote_copy(
            src_ref=src, dst_ref=dst, send_sem=s, recv_sem=r,
            device_id=target, device_id_type=pl.DeviceIdType.MESH,
        )

    def lower_copy(j):
        return remote(
            d_hbm.at[:, pl.ds(2 * T * j, 2 * T)], lower.at[hi, j], send_l.at[j], recv_l.at[j], to_pair_l
        )

    def lower_arrived(j):
        remote(lower.at[1 - hi, j], lower.at[1 - hi, j], send_l.at[j], recv_l.at[j], to_pair_l).wait_recv()

    for j in range(planes):
        @pl.when(z == j)
        def _():
            lower_copy(j).start()
    z_copy = remote(z_hbm, zbuf.at[hi], send_z.at[0], recv_z.at[0], to_pair_z)
    z_copy.start()
    for j in range(planes):
        @pl.when(z > j)
        def _():
            lower_copy(j).start()

    pending = []
    arrived = set()

    def span(p):
        return pl.ds(p * piece_rows, piece_rows)

    def send_panel(src, slot, p, target):
        c = remote(src, panel.at[slot, span(p)], send_a.at[len(pending)], recv_a.at[slot, p], target)
        c.start()
        pending.append(c)

    slots = {
        (side, where): place(side_lo, where_x, core)
        for side, side_lo in (("own", lo), ("other", 1 - lo))
        for where, where_x in (("here", x), ("prev", x_prev), ("next", x_next), ("far", x_far))
    }

    def wait_panel(slot, p):
        view = panel.at[slot, span(p)]
        remote(view, view, send_a.at[0], recv_a.at[slot, p], to_sibling).wait_recv()

    def receive(key, p):
        if (key, p) in arrived:
            return
        arrived.add((key, p))
        slot = slots[key]
        wait_panel(slot, p)
        send_panel(panel.at[slot, span(p)], slot, p, to_sibling)

    def forward(key, p, target):
        receive(key, p)
        slot = slots[key]
        send_panel(panel.at[slot, span(p)], slot, p, target)

    for p, q in zip((0, 2, 1, 3), (2, 3, 0, 1)):
        send_panel(a_hbm.at[span(p)], col, p, to_x_next)
        send_panel(a_hbm.at[span(p)], col, p, to_x_prev)
        send_panel(a_hbm.at[span(q)], col, q, to_y)
        send_panel(a_hbm.at[span(p)], col, p, to_sibling)

    def relay_1():
        forward(("own", "prev"), 0, to_x_next)
        forward(("own", "prev"), 0, to_y)
        forward(("own", "next"), 0, to_y)
        forward(("other", "here"), 2, to_x_next)
        forward(("other", "here"), 2, to_x_prev)

    def relay_2():
        forward(("own", "next"), 1, to_x_prev)
        forward(("other", "here"), 3, to_x_next)
        forward(("other", "here"), 3, to_x_prev)
        forward(("own", "prev"), 1, to_y)
        forward(("own", "next"), 1, to_y)

    def relay_3():
        forward(("own", "prev"), 2, to_x_next)
        forward(("own", "next"), 3, to_x_prev)

    def relay_4():
        forward(("own", "far"), 0, to_y)
        forward(("own", "far"), 1, to_y)

    def relay_5():
        forward(("other", "prev"), 2, to_x_next)
        forward(("other", "next"), 3, to_x_prev)

    relays = {1: relay_1, 3: relay_2, 4: relay_3, 5: relay_4, 6: relay_5}

    for c in own_copies:
        c.wait()
    z_copy.wait_send()
    remote(zbuf.at[1 - hi], zbuf.at[1 - hi], send_z.at[0], recv_z.at[0], to_pair_z).wait_recv()
    for j in range(planes):
        @pl.when(z == j)
        def _():
            lower_arrived(j)
    acc[...] = zbuf[...].reshape(2 * T, T)
    first_rows = lower[0, z]
    second_rows = lower[1, z]
    inv_a, inv_b = invert_lower([first_rows[:, :T], second_rows[:, T:]])
    inverse[0] = left_form(inv_a)
    inverse[1] = left_form(inv_b)
    inverse[2] = left_form(second_rows[:, :T])

    def solved_copy(k, half, target, way):
        view = solved.at[2 * k + half]
        return remote(view, view, send_s.at[way, 2 * k + half], recv_s.at[2 * k + half], target)

    for k in range(planes):
        dist = (z - k + planes) % planes
        goes_next = dist <= 3
        goes_prev = (dist == 0) | (dist >= 6)

        def spread(half):
            @pl.when(goes_next)
            def _():
                solved_copy(k, half, to_z_next, 0).start()

            @pl.when(goes_prev)
            def _():
                solved_copy(k, half, to_z_prev, 1).start()

        @pl.when(dist == 0)
        def _():
            s_a = product(inverse[0], right_form(acc[:T]))
            solved[2 * k] = s_a
            spread(0)
            rest = acc[T:] - product(inverse[2], right_form(s_a))
            solved[2 * k + 1] = product(inverse[1], right_form(rest))
            spread(1)

        @pl.when(dist != 0)
        def _():
            @pl.when(z > k)
            def _():
                lower_arrived(k)

            tile = lower[:, k].reshape(2 * T, 2 * T)
            for half in range(2):
                solved_copy(k, half, to_z_next, 0).wait_recv()
                spread(half)

                @pl.when(z > k)
                def _():
                    acc[...] -= product(
                        left_form(tile[:, half * T:(half + 1) * T]), right_form(solved[2 * k + half])
                    )

        if k in relays:
            relays[k]()

    for p in range(PIECES):
        for key in slots:
            if key != ("own", "here"):
                receive(key, p)
    for p in range(PIECES):
        for lo_ in range(2):
            for x_ in range(4):
                wait_panel(place(lo_, x_, 1 - core), p)

    total = norm_ref[...]
    for k in range(2 * planes):
        block = solved[k]
        total = total + jnp.sum(block * block, axis=0, keepdims=True)
        solved_right[k] = right_form(block)
    norm_out[...] = total

    tile_rows = 512

    def multiply(i, carry):
        pair, t = i // (height // tile_rows), i % (height // tile_rows)
        part = pl.ds(pl.multiple_of(t * tile_rows, tile_rows), tile_rows)
        left = jnp.concatenate([left_form(panel[2 * pair, part]), left_form(panel[2 * pair + 1, part])], axis=1)
        right = solved_right[pl.ds(2 * pair, 2)].reshape(4 * T, 2 * T)
        value = product(left, right)

        @pl.when(pair == 0)
        def _():
            update_ref[part] = value

        @pl.when(pair > 0)
        def _():
            update_ref[part] += value

        return carry

    lax.fori_loop(0, planes * (height // tile_rows), multiply, 0)

    for c in pending:
        c.wait_send()
    for j in range(planes):
        @pl.when(z >= j)
        def _():
            lower_copy(j).wait_send()
    for k in range(planes):
        dist = (z - k + planes) % planes
        for half in range(2):
            @pl.when(dist <= 3)
            def _():
                solved_copy(k, half, to_z_next, 0).wait_send()

            @pl.when((dist == 0) | (dist >= 6))
            def _():
                solved_copy(k, half, to_z_prev, 1).wait_send()


def shards(diag_block, z_panel, panel_below, z_trail, norm_sq):
    height = panel_below.shape[0]
    dma = pltpu.SemaphoreType.DMA
    norm_out, update = pl.pallas_call(
        kernel,
        out_shape=(
            jax.ShapeDtypeStruct((1, T), F32),
            jax.ShapeDtypeStruct((height, T), F32),
        ),
        in_specs=[pl.BlockSpec(memory_space=pl.ANY)] * 3 + [pl.BlockSpec(memory_space=pltpu.VMEM)],
        out_specs=(pl.BlockSpec(memory_space=pltpu.VMEM),) * 2,
        scratch_shapes=[
            pltpu.VMEM((16, height, T), F32),
            pltpu.VMEM((2, 8, T, 2 * T), F32),
            pltpu.VMEM((2, T, T), F32),
            pltpu.VMEM((2 * T, T), F32),
            pltpu.VMEM((16, T, T), F32),
            pltpu.VMEM((16, 2 * T, 2 * T), BF16),
            pltpu.VMEM((3, T, 2 * T), BF16),
            dma((10,)), dma((64,)), dma((16, PIECES)), dma((8,)), dma((8,)),
            dma((1,)), dma((1,)), dma((2, 16)), dma((16,)),
        ],
        compiler_params=pltpu.CompilerParams(
            collective_id=0, has_side_effects=True, vmem_limit_bytes=48 * 1024 * 1024
        ),
        name="panel_update",
    )(diag_block, z_panel, panel_below, norm_sq.reshape(1, T))
    return norm_out.reshape(T), z_trail - update


def solution(mesh):
    return jax.shard_map(
        shards,
        mesh=mesh,
        in_specs=(P("row", None), P("row", "col"), P("row", "col"), P("row", "col"), P("col")),
        out_specs=(P("col"), P("row", "col")),
        check_vma=False,
    )
```

```python
import jax
import jax.numpy as jnp
from jax import lax
from jax.experimental import pallas as pl
from jax.experimental.pallas import tpu as pltpu
from jax.sharding import PartitionSpec as P

F32 = jnp.float32
BF16 = jnp.bfloat16
T = 128
PIECES = 4


def halves(v):
    high = v.astype(BF16)
    low = (v - high.astype(F32)).astype(BF16)
    return high, low


def left_form(v):
    high, low = halves(v)
    return jnp.concatenate([high, low], axis=1)


def right_form(v):
    high, low = halves(v)
    both = jnp.concatenate([high, low], axis=1)
    return jnp.concatenate([both, both], axis=0)


def product(left, right):
    wide = jnp.dot(left, right, preferred_element_type=F32)
    return wide[:, :T] + wide[:, T:]


def invert_lower(blocks):
    rows = lax.broadcasted_iota(jnp.int32, (T, T), 0)
    cols = lax.broadcasted_iota(jnp.int32, (T, T), 1)
    on_diag = rows == cols
    found = [jnp.where(on_diag, 1.0 / jnp.where(on_diag, b, 1.0), 0.0) for b in blocks]
    size = 1
    while size < T:
        below = (
            (rows // (2 * size) == cols // (2 * size))
            & ((rows // size) % 2 == 1)
            & ((cols // size) % 2 == 0)
        )
        offs = [jnp.where(below, b, 0.0) for b in blocks]
        mids = [product(left_form(o), right_form(x)) for o, x in zip(offs, found)]
        found = [x - product(left_form(x), right_form(m)) for x, m in zip(found, mids)]
        size *= 2
    return found


def kernel(
    d_hbm, z_hbm, a_hbm, norm_ref,
    norm_out, update_ref,
    panel, lower, zbuf, acc, solved, solved_right, inverse,
    own_sem, send_a, recv_a, send_l, recv_l, send_z, recv_z, send_s, recv_s,
):
    row = lax.axis_index("row")
    col = lax.axis_index("col")
    z, hi = row // 2, row % 2
    lo, x, core = col // 8, (col // 2) % 4, col % 2
    height = a_hbm.shape[0]
    piece_rows = height // PIECES
    planes = 8

    def place(lo_, x_, core_):
        return lo_ * 8 + x_ * 2 + core_

    x_next, x_prev, x_far = (x + 1) % 4, (x + 3) % 4, (x + 2) % 4
    to_x_next = {"row": row, "col": place(lo, x_next, core)}
    to_x_prev = {"row": row, "col": place(lo, x_prev, core)}
    to_y = {"row": row, "col": place(1 - lo, x, core)}
    to_sibling = {"row": row, "col": place(lo, x, 1 - core)}
    to_pair_l = {"row": z * 2 + 1 - hi, "col": place(1 - lo, x, core)}
    to_pair_z = {"row": z * 2 + 1 - hi, "col": col}
    to_z_next = {"row": ((z + 1) % planes) * 2 + hi, "col": col}
    to_z_prev = {"row": ((z + planes - 1) % planes) * 2 + hi, "col": col}
    partners = [to_x_next, to_x_prev, to_y, to_sibling, to_pair_l, to_pair_z, to_z_next, to_z_prev]

    own_copies = [pltpu.make_async_copy(a_hbm, panel.at[col], own_sem.at[0])]
    own_copies.append(pltpu.make_async_copy(z_hbm, zbuf.at[hi], own_sem.at[1]))
    for j in range(planes):
        own_copies.append(
            pltpu.make_async_copy(d_hbm.at[:, pl.ds(2 * T * j, 2 * T)], lower.at[hi, j], own_sem.at[2 + j])
        )
    for c in own_copies:
        c.start()

    barrier = pltpu.get_barrier_semaphore()
    for d in partners:
        pl.semaphore_signal(barrier, inc=1, device_id=d, device_id_type=pl.DeviceIdType.MESH)
    pl.semaphore_wait(barrier, len(partners))

    def remote(src, dst, s, r, target):
        return pltpu.make_async_remote_copy(
            src_ref=src, dst_ref=dst, send_sem=s, recv_sem=r,
            device_id=target, device_id_type=pl.DeviceIdType.MESH,
        )

    def lower_copy(j):
        return remote(
            d_hbm.at[:, pl.ds(2 * T * j, 2 * T)], lower.at[hi, j], send_l.at[j], recv_l.at[j], to_pair_l
        )

    def lower_arrived(j):
        remote(lower.at[1 - hi, j], lower.at[1 - hi, j], send_l.at[j], recv_l.at[j], to_pair_l).wait_recv()

    for j in range(planes):
        @pl.when(z == j)
        def _():
            lower_copy(j).start()
    z_copy = remote(z_hbm, zbuf.at[hi], send_z.at[0], recv_z.at[0], to_pair_z)
    z_copy.start()
    for j in range(planes):
        @pl.when(z > j)
        def _():
            lower_copy(j).start()

    pending = []
    arrived = set()

    def span(p):
        return pl.ds(p * piece_rows, piece_rows)

    def send_panel(src, slot, p, target):
        c = remote(src, panel.at[slot, span(p)], send_a.at[len(pending)], recv_a.at[slot, p], target)
        c.start()
        pending.append(c)

    slots = {
        (side, where): place(side_lo, where_x, core)
        for side, side_lo in (("own", lo), ("other", 1 - lo))
        for where, where_x in (("here", x), ("prev", x_prev), ("next", x_next), ("far", x_far))
    }

    def wait_panel(slot, p):
        view = panel.at[slot, span(p)]
        remote(view, view, send_a.at[0], recv_a.at[slot, p], to_sibling).wait_recv()

    def receive(key, p):
        if (key, p) in arrived:
            return
        arrived.add((key, p))
        slot = slots[key]
        wait_panel(slot, p)
        send_panel(panel.at[slot, span(p)], slot, p, to_sibling)

    def forward(key, p, target):
        receive(key, p)
        slot = slots[key]
        send_panel(panel.at[slot, span(p)], slot, p, target)

    for p, q, y in zip((0, 2, 1, 3), (1, 3, 0, 2), (2, 3, 0, 1)):
        send_panel(a_hbm.at[span(p)], col, p, to_x_next)
        send_panel(a_hbm.at[span(q)], col, q, to_x_prev)
        send_panel(a_hbm.at[span(y)], col, y, to_y)
        send_panel(a_hbm.at[span(p)], col, p, to_sibling)

    prev, following, far = ("own", "prev"), ("own", "next"), ("own", "far")
    across, across_prev, across_next = ("other", "here"), ("other", "prev"), ("other", "next")
    relays = {
        1: (
            [(prev, 0, to_x_next), (following, 1, to_x_prev), (across, 2, to_x_next),
             (prev, 0, to_y), (following, 1, to_y)],
            [],
        ),
        2: (
            [(across, 3, to_x_prev), (across, 2, to_x_prev), (across, 3, to_x_next),
             (prev, 2, to_x_next), (following, 3, to_x_prev)],
            [],
        ),
        3: ([(prev, 1, to_y), (following, 0, to_y)], [(across, 0)]),
        4: ([(far, 0, to_y), (far, 1, to_y)], [(prev, 3), (following, 2), (across, 1)]),
        5: ([(across_prev, 2, to_x_next), (across_next, 3, to_x_prev)], [(across_prev, 0)]),
        6: ([], [(across_prev, 3), (across_next, 2), (across_next, 1), (across_prev, 1)]),
    }

    def relay(k):
        onward, taken = relays.get(k, ([], []))
        for key, p, target in onward:
            forward(key, p, target)
        for key, p in taken:
            receive(key, p)

    sibling_taken = set()

    def wait_sibling(key):
        if key in sibling_taken:
            return
        sibling_taken.add(key)
        for p in range(PIECES):
            wait_panel(slots[key] + 1 - 2 * core, p)

    tile_rows = 512
    chip = lo * 4 + x

    def multiply(pair):
        right = solved_right[pl.ds(2 * pair, 2)].reshape(4 * T, 2 * T)

        def tile(t, carry):
            part = pl.ds(pl.multiple_of(t * tile_rows, tile_rows), tile_rows)
            left = jnp.concatenate(
                [left_form(panel[2 * pair, part]), left_form(panel[2 * pair + 1, part])], axis=1
            )
            update_ref[part] += product(left, right)
            return carry

        lax.fori_loop(0, height // tile_rows, tile, 0)

    def step_of(pair):
        same_plane = pair // 4 == lo
        apart = (pair % 4 - x + 4) % 4
        near = jnp.where(same_plane, apart != 2, apart == 0)
        here = same_plane & (apart == 0)
        phase = jnp.where(here, 1, jnp.where(near, 5, planes))
        due = jnp.maximum(pair, phase)
        return due + jnp.where(z == due + 1, 1, 0)

    def multiply_due(k):
        def one(pair, carry):
            @pl.when(step_of(pair) == k)
            def _():
                multiply(pair)

            return carry

        lax.fori_loop(0, planes, one, 0)

    for c in own_copies:
        c.wait()
    z_copy.wait_send()
    remote(zbuf.at[1 - hi], zbuf.at[1 - hi], send_z.at[0], recv_z.at[0], to_pair_z).wait_recv()
    for j in range(planes):
        @pl.when(z == j)
        def _():
            lower_arrived(j)
    acc[...] = zbuf[...].reshape(2 * T, T)
    update_ref[...] = jnp.zeros_like(update_ref)
    first_rows = lower[0, z]
    second_rows = lower[1, z]
    inv_a, inv_b = invert_lower([first_rows[:, :T], second_rows[:, T:]])
    inverse[0] = left_form(inv_a)
    inverse[1] = left_form(inv_b)
    inverse[2] = left_form(second_rows[:, :T])

    def solved_copy(k, half, target, way):
        view = solved.at[2 * k + half]
        return remote(view, view, send_s.at[way, 2 * k + half], recv_s.at[2 * k + half], target)

    for k in range(planes):
        dist = (z - k + planes) % planes
        goes_next = dist <= 3
        goes_prev = (dist == 0) | (dist >= 6)

        def spread(half):
            @pl.when(goes_next)
            def _():
                solved_copy(k, half, to_z_next, 0).start()

            @pl.when(goes_prev)
            def _():
                solved_copy(k, half, to_z_prev, 1).start()

        @pl.when(dist == 0)
        def _():
            s_a = product(inverse[0], right_form(acc[:T]))
            solved[2 * k] = s_a
            spread(0)
            rest = acc[T:] - product(inverse[2], right_form(s_a))
            solved[2 * k + 1] = product(inverse[1], right_form(rest))
            spread(1)

        @pl.when(dist != 0)
        def _():
            @pl.when(z > k)
            def _():
                lower_arrived(k)

            tile = lower[:, k].reshape(2 * T, 2 * T)
            for half in range(2):
                solved_copy(k, half, to_z_next, 0).wait_recv()
                spread(half)

                @pl.when(z > k)
                def _():
                    acc[...] -= product(
                        left_form(tile[:, half * T:(half + 1) * T]), right_form(solved[2 * k + half])
                    )

        for half in range(2):
            solved_right[2 * k + half] = right_form(solved[2 * k + half])
        relay(k)
        if k == 1:
            wait_sibling(("own", "here"))
        if k == 5:
            for key in (prev, following, across):
                wait_sibling(key)
        if k >= 1:
            multiply_due(k)

    for p in range(PIECES):
        for key in slots:
            if key != ("own", "here"):
                receive(key, p)
    for key in slots:
        wait_sibling(key)
    multiply_due(planes)
    total = norm_ref[...]
    for k in range(2 * planes):
        block = solved[k]
        total = total + jnp.sum(block * block, axis=0, keepdims=True)
    norm_out[...] = total

    for c in pending:
        c.wait_send()
    for j in range(planes):
        @pl.when(z >= j)
        def _():
            lower_copy(j).wait_send()
    for k in range(planes):
        dist = (z - k + planes) % planes
        for half in range(2):
            @pl.when(dist <= 3)
            def _():
                solved_copy(k, half, to_z_next, 0).wait_send()

            @pl.when((dist == 0) | (dist >= 6))
            def _():
                solved_copy(k, half, to_z_prev, 1).wait_send()


def shards(diag_block, z_panel, panel_below, z_trail, norm_sq):
    height = panel_below.shape[0]
    dma = pltpu.SemaphoreType.DMA
    norm_out, update = pl.pallas_call(
        kernel,
        out_shape=(
            jax.ShapeDtypeStruct((1, T), F32),
            jax.ShapeDtypeStruct((height, T), F32),
        ),
        in_specs=[pl.BlockSpec(memory_space=pl.ANY)] * 3 + [pl.BlockSpec(memory_space=pltpu.VMEM)],
        out_specs=(pl.BlockSpec(memory_space=pltpu.VMEM),) * 2,
        scratch_shapes=[
            pltpu.VMEM((16, height, T), F32),
            pltpu.VMEM((2, 8, T, 2 * T), F32),
            pltpu.VMEM((2, T, T), F32),
            pltpu.VMEM((2 * T, T), F32),
            pltpu.VMEM((16, T, T), F32),
            pltpu.VMEM((16, 2 * T, 2 * T), BF16),
            pltpu.VMEM((3, T, 2 * T), BF16),
            dma((10,)), dma((64,)), dma((16, PIECES)), dma((8,)), dma((8,)),
            dma((1,)), dma((1,)), dma((2, 16)), dma((16,)),
        ],
        compiler_params=pltpu.CompilerParams(
            collective_id=0, has_side_effects=True, vmem_limit_bytes=67_043_328
        ),
        name="panel_update",
    )(diag_block, z_panel, panel_below, norm_sq.reshape(1, T))
    return norm_out.reshape(T), z_trail - update


def solution(mesh):
    return jax.shard_map(
        shards,
        mesh=mesh,
        in_specs=(P("row", None), P("row", "col"), P("row", "col"), P("row", "col"), P("col")),
        out_specs=(P("col"), P("row", "col")),
        check_vma=False,
    )
```

```python
import jax
import jax.numpy as jnp
from jax import lax
from jax.experimental import pallas as pl
from jax.experimental.pallas import tpu as pltpu
from jax.sharding import PartitionSpec as P

F32 = jnp.float32
BF16 = jnp.bfloat16
T = 128
PIECES = 4


def halves(v):
    high = v.astype(BF16)
    low = (v - high.astype(F32)).astype(BF16)
    return high, low


def left_form(v):
    high, low = halves(v)
    return jnp.concatenate([high, low], axis=1)


def right_form(v):
    high, low = halves(v)
    both = jnp.concatenate([high, low], axis=1)
    return jnp.concatenate([both, both], axis=0)


def product(left, right):
    wide = jnp.dot(left, right, preferred_element_type=F32)
    return wide[:, :T] + wide[:, T:]


def invert_lower(blocks):
    rows = lax.broadcasted_iota(jnp.int32, (T, T), 0)
    cols = lax.broadcasted_iota(jnp.int32, (T, T), 1)
    on_diag = rows == cols
    found = [jnp.where(on_diag, 1.0 / jnp.where(on_diag, b, 1.0), 0.0) for b in blocks]
    size = 1
    while size < T:
        below = (
            (rows // (2 * size) == cols // (2 * size))
            & ((rows // size) % 2 == 1)
            & ((cols // size) % 2 == 0)
        )
        offs = [jnp.where(below, b, 0.0) for b in blocks]
        mids = [product(left_form(o), right_form(x)) for o, x in zip(offs, found)]
        found = [x - product(left_form(x), right_form(m)) for x, m in zip(found, mids)]
        size *= 2
    return found


def relay_table(planes):
    windows = ((9.5, 21.0), (15.0, 21.0), (21.0, 33.0), (31.0, 43.0), (36.5, 43.0), (48.0, 55.0))
    starts = (6.4, 4.7, 2.2, 0.0, 7.4, 10.5, 14.1, 12.3)

    def reached(k, z):
        apart = (z - k) % planes
        return 14.4 + 5.4 * k + 3.1 * min(apart, planes - apart)

    table, first = [], [0] * planes
    for ready, limit in windows:
        steps = []
        for z in range(planes):
            there = ready + starts[z] + 3.0
            slack = 0.8 * (max(starts) - starts[z])

            def cost(k):
                when = reached(k, z)
                late = 0.3 * max(when - there, 0.0) + max(when - limit - starts[z] - slack, 0.0)
                if k < z - 1:
                    late += 6.0 * max(there + 1.0 - reached(z - 1, z), 0.0)
                return late + 0.3 * max(there - when, 0.0)

            steps.append(min(range(first[z], planes), key=cost))
        first = steps
        table.append(steps)
    return table


def kernel(
    d_hbm, z_hbm, a_hbm, norm_ref,
    norm_out, update_ref,
    panel, lower, zbuf, acc, solved, solved_right, inverse,
    own_sem, send_a, recv_a, send_l, recv_l, send_z, recv_z, send_s, recv_s,
):
    row = lax.axis_index("row")
    col = lax.axis_index("col")
    z, hi = row // 2, row % 2
    lo, x, core = col // 8, (col // 2) % 4, col % 2
    height = a_hbm.shape[0]
    piece_rows = height // PIECES
    planes = 8

    def place(lo_, x_, core_):
        return lo_ * 8 + x_ * 2 + core_

    x_next, x_prev, x_far = (x + 1) % 4, (x + 3) % 4, (x + 2) % 4
    to_x_next = {"row": row, "col": place(lo, x_next, core)}
    to_x_prev = {"row": row, "col": place(lo, x_prev, core)}
    to_y = {"row": row, "col": place(1 - lo, x, core)}
    to_sibling = {"row": row, "col": place(lo, x, 1 - core)}
    to_pair_l = {"row": z * 2 + 1 - hi, "col": place(1 - lo, x, core)}
    to_pair_z = {"row": z * 2 + 1 - hi, "col": col}
    to_z_next = {"row": ((z + 1) % planes) * 2 + hi, "col": col}
    to_z_prev = {"row": ((z + planes - 1) % planes) * 2 + hi, "col": col}
    partners = [to_x_next, to_x_prev, to_y, to_sibling, to_pair_l, to_pair_z, to_z_next, to_z_prev]

    own_copies = [pltpu.make_async_copy(a_hbm, panel.at[col], own_sem.at[0])]
    own_copies.append(pltpu.make_async_copy(z_hbm, zbuf.at[hi], own_sem.at[1]))
    for j in range(planes):
        own_copies.append(
            pltpu.make_async_copy(d_hbm.at[:, pl.ds(2 * T * j, 2 * T)], lower.at[hi, j], own_sem.at[2 + j])
        )
    for c in own_copies:
        c.start()

    barrier = pltpu.get_barrier_semaphore()
    for d in partners:
        pl.semaphore_signal(barrier, inc=1, device_id=d, device_id_type=pl.DeviceIdType.MESH)
    pl.semaphore_wait(barrier, len(partners))

    def remote(src, dst, s, r, target):
        return pltpu.make_async_remote_copy(
            src_ref=src, dst_ref=dst, send_sem=s, recv_sem=r,
            device_id=target, device_id_type=pl.DeviceIdType.MESH,
        )

    def lower_copy(j):
        return remote(
            d_hbm.at[:, pl.ds(2 * T * j, 2 * T)], lower.at[hi, j], send_l.at[j], recv_l.at[j], to_pair_l
        )

    def lower_arrived(j):
        remote(lower.at[1 - hi, j], lower.at[1 - hi, j], send_l.at[j], recv_l.at[j], to_pair_l).wait_recv()

    for j in range(planes):
        @pl.when(z == j)
        def _():
            lower_copy(j).start()
    z_copy = remote(z_hbm, zbuf.at[hi], send_z.at[0], recv_z.at[0], to_pair_z)
    z_copy.start()
    for j in range(planes):
        @pl.when(z > j)
        def _():
            lower_copy(j).start()

    pending = []

    def span(p):
        return pl.ds(p * piece_rows, piece_rows)

    def panel_copy(src, slot, p, index, target):
        return remote(src, panel.at[slot, span(p)], send_a.at[index], recv_a.at[slot, p], target)

    def send_own(p, target):
        panel_copy(a_hbm.at[span(p)], col, p, len(pending), target).start()
        pending.append((col, p, target))

    slots = {
        (side, where): place(side_lo, where_x, core)
        for side, side_lo in (("own", lo), ("other", 1 - lo))
        for where, where_x in (("here", x), ("prev", x_prev), ("next", x_next), ("far", x_far))
    }

    def wait_panel(slot, p):
        view = panel.at[slot, span(p)]
        remote(view, view, send_a.at[0], recv_a.at[slot, p], to_sibling).wait_recv()

    for p, q, y in zip((0, 2, 1, 3), (1, 3, 0, 2), (2, 3, 0, 1)):
        send_own(p, to_x_next)
        send_own(q, to_x_prev)
        send_own(y, to_y)
        send_own(p, to_sibling)

    prev, following, far = ("own", "prev"), ("own", "next"), ("own", "far")
    across, across_prev, across_next = ("other", "here"), ("other", "prev"), ("other", "next")
    every = range(PIECES)
    groups = [
        (
            [(prev, 0, to_x_next), (following, 1, to_x_prev), (across, 2, to_x_next),
             (prev, 0, to_y), (following, 1, to_y)],
            [], [("own", "here")],
        ),
        (
            [(across, 3, to_x_prev), (across, 2, to_x_prev), (across, 3, to_x_next),
             (prev, 2, to_x_next), (following, 3, to_x_prev)],
            [], [],
        ),
        ([(prev, 1, to_y), (following, 0, to_y)], [(across, 0)], []),
        ([(far, 0, to_y), (far, 1, to_y)], [(prev, 3), (following, 2), (across, 1)], []),
        (
            [(across_prev, 2, to_x_next), (across_next, 3, to_x_prev)],
            [(across_prev, 0), (across_next, 1)], [prev, following, across],
        ),
        (
            [], [(across_prev, 3), (across_next, 2), (across_prev, 1), (far, 2), (far, 3)],
            [far, across_prev],
        ),
        ([], [(("other", "far"), p) for p in (0, 2, 3, 1)] + [(across_next, 0)], [across_next, ("other", "far")]),
    ]
    plans = []
    arrived = set()
    for onward, taken, beside in groups:
        plan = []
        for key, p, target in onward + [(key, p, None) for key, p in taken]:
            if (key, p) not in arrived:
                arrived.add((key, p))
                plan.append((slots[key], p, None, None))
                plan.append((slots[key], p, len(pending), to_sibling))
                pending.append((slots[key], p, to_sibling))
            if target is not None:
                plan.append((slots[key], p, len(pending), target))
                pending.append((slots[key], p, target))
        plans.append((plan, beside))

    def relay(group):
        plan, beside = plans[group]
        for slot, p, index, target in plan:
            if target is None:
                wait_panel(slot, p)
            else:
                panel_copy(panel.at[slot, span(p)], slot, p, index, target).start()
        for key in beside:
            for p in every:
                wait_panel(slots[key] + 1 - 2 * core, p)

    relay_steps = relay_table(planes)

    def by_plane(values):
        picked = jnp.int32(values[0])
        for v in range(1, planes):
            picked = jnp.where(z == v, values[v], picked)
        return picked

    def relay_due(k):
        for group, steps in enumerate(relay_steps):
            here = [v for v in range(planes) if steps[v] == k]
            if len(here) == planes:
                relay(group)
            elif here:
                chosen = z == here[0]
                for v in here[1:]:
                    chosen = chosen | (z == v)

                @pl.when(chosen)
                def _():
                    relay(group)

    tile_rows = 512
    chip = lo * 4 + x

    def multiply(pair):
        right = solved_right[pl.ds(2 * pair, 2)].reshape(4 * T, 2 * T)

        for t in range(height // tile_rows):
            part = pl.ds(t * tile_rows, tile_rows)
            left = jnp.concatenate(
                [left_form(panel[2 * pair, part]), left_form(panel[2 * pair + 1, part])], axis=1
            )
            update_ref[part] += product(left, right)

    def step_of(pair):
        same_plane = pair // 4 == lo
        apart = (pair % 4 - x + 4) % 4
        near = jnp.where(same_plane, apart != 2, apart == 0)
        middle = jnp.where(same_plane, apart == 2, apart == 3)
        here = same_plane & (apart == 0)
        phase = jnp.where(middle, by_plane(relay_steps[5]), planes)
        phase = jnp.where(near, by_plane(relay_steps[4]), phase)
        phase = jnp.where(here, by_plane(relay_steps[0]), phase)
        due = jnp.maximum(pair, phase)
        return due

    def multiply_due(k):
        def one(pair, carry):
            @pl.when(step_of(pair) == k)
            def _():
                multiply(pair)

            return carry

        lax.fori_loop(0, planes, one, 0)

    for c in own_copies:
        c.wait()
    z_copy.wait_send()
    remote(zbuf.at[1 - hi], zbuf.at[1 - hi], send_z.at[0], recv_z.at[0], to_pair_z).wait_recv()
    for j in range(planes):
        @pl.when(z == j)
        def _():
            lower_arrived(j)
    acc[...] = zbuf[...].reshape(2 * T, T)
    update_ref[...] = jnp.zeros_like(update_ref)
    first_rows = lower[0, z]
    second_rows = lower[1, z]
    inv_a, inv_b = invert_lower([first_rows[:, :T], second_rows[:, T:]])
    inverse[0] = left_form(inv_a)
    inverse[1] = left_form(inv_b)
    inverse[2] = left_form(second_rows[:, :T])

    def solved_copy(k, half, target, way):
        view = solved.at[2 * k + half]
        return remote(view, view, send_s.at[way, 2 * k + half], recv_s.at[2 * k + half], target)

    def spread(k, half):
        dist = (z - k + planes) % planes

        @pl.when(dist <= 3)
        def _():
            solved_copy(k, half, to_z_next, 0).start()

        @pl.when((dist == 0) | (dist >= 6))
        def _():
            solved_copy(k, half, to_z_prev, 1).start()

    def solve_own(k, rest_a, rest_b):
        s_a = product(inverse[0], right_form(rest_a))
        solved[2 * k] = s_a
        spread(k, 0)
        solved[2 * k + 1] = product(inverse[1], right_form(rest_b() - product(inverse[2], right_form(s_a))))
        spread(k, 1)

    @pl.when(z == 0)
    def _():
        solve_own(0, acc[:T], lambda: acc[T:])

    for k in range(planes):
        @pl.when(z > k)
        def _():
            lower_arrived(k)
            tile = lower[:, k].reshape(2 * T, 2 * T)
            solved_copy(k, 0, to_z_next, 0).wait_recv()
            spread(k, 0)
            acc[...] -= product(left_form(tile[:, :T]), right_form(solved[2 * k]))
            solved_copy(k, 1, to_z_next, 0).wait_recv()
            spread(k, 1)
            right = right_form(solved[2 * k + 1])

            @pl.when(z == k + 1)
            def _():
                if k + 1 < planes:
                    solve_own(
                        k + 1,
                        acc[:T] - product(left_form(tile[:T, T:]), right),
                        lambda: acc[T:] - product(left_form(tile[T:, T:]), right),
                    )

            @pl.when(z > k + 1)
            def _():
                acc[...] -= product(left_form(tile[:, T:]), right)

        @pl.when(z < k)
        def _():
            for half in range(2):
                solved_copy(k, half, to_z_next, 0).wait_recv()
                spread(k, half)

        for half in range(2):
            solved_right[2 * k + half] = right_form(solved[2 * k + half])
        relay_due(k)
        multiply_due(k)

    relay(len(groups) - 1)
    multiply_due(planes)
    total = norm_ref[...]
    for k in range(2 * planes):
        block = solved[k]
        total = total + jnp.sum(block * block, axis=0, keepdims=True)
    norm_out[...] = total

    for index, (slot, p, target) in enumerate(pending):
        panel_copy(panel.at[slot, span(p)], slot, p, index, target).wait_send()
    for j in range(planes):
        @pl.when(z >= j)
        def _():
            lower_copy(j).wait_send()
    for k in range(planes):
        dist = (z - k + planes) % planes
        for half in range(2):
            @pl.when(dist <= 3)
            def _():
                solved_copy(k, half, to_z_next, 0).wait_send()

            @pl.when((dist == 0) | (dist >= 6))
            def _():
                solved_copy(k, half, to_z_prev, 1).wait_send()


def shards(diag_block, z_panel, panel_below, z_trail, norm_sq):
    height = panel_below.shape[0]
    dma = pltpu.SemaphoreType.DMA
    norm_out, update = pl.pallas_call(
        kernel,
        out_shape=(
            jax.ShapeDtypeStruct((1, T), F32),
            jax.ShapeDtypeStruct((height, T), F32),
        ),
        in_specs=[pl.BlockSpec(memory_space=pl.ANY)] * 3 + [pl.BlockSpec(memory_space=pltpu.VMEM)],
        out_specs=(pl.BlockSpec(memory_space=pltpu.VMEM),) * 2,
        scratch_shapes=[
            pltpu.VMEM((16, height, T), F32),
            pltpu.VMEM((2, 8, T, 2 * T), F32),
            pltpu.VMEM((2, T, T), F32),
            pltpu.VMEM((2 * T, T), F32),
            pltpu.VMEM((16, T, T), F32),
            pltpu.VMEM((16, 2 * T, 2 * T), BF16),
            pltpu.VMEM((3, T, 2 * T), BF16),
            dma((10,)), dma((64,)), dma((16, PIECES)), dma((8,)), dma((8,)),
            dma((1,)), dma((1,)), dma((2, 16)), dma((16,)),
        ],
        compiler_params=pltpu.CompilerParams(
            collective_id=0, has_side_effects=True, vmem_limit_bytes=67_043_328
        ),
        name="panel_update",
    )(diag_block, z_panel, panel_below, norm_sq.reshape(1, T))
    return norm_out.reshape(T), z_trail - update


def solution(mesh):
    return jax.shard_map(
        shards,
        mesh=mesh,
        in_specs=(P("row", None), P("row", "col"), P("row", "col"), P("row", "col"), P("col")),
        out_specs=(P("col"), P("row", "col")),
        check_vma=False,
    )
```

```python
import jax
import jax.numpy as jnp
from jax import lax
from jax.experimental import pallas as pl
from jax.experimental.pallas import tpu as pltpu
from jax.sharding import PartitionSpec as P

F32 = jnp.float32
BF16 = jnp.bfloat16
T = 128
PIECES = 4


def halves(v):
    high = v.astype(BF16)
    low = (v - high.astype(F32)).astype(BF16)
    return high, low


def left_form(v):
    high, low = halves(v)
    return jnp.concatenate([high, low], axis=1)


def right_form(v):
    high, low = halves(v)
    both = jnp.concatenate([high, low], axis=1)
    return jnp.concatenate([both, both], axis=0)


def product(left, right):
    wide = jnp.dot(left, right, preferred_element_type=F32)
    return wide[:, :T] + wide[:, T:]


def invert_lower(blocks):
    rows = lax.broadcasted_iota(jnp.int32, (T, T), 0)
    cols = lax.broadcasted_iota(jnp.int32, (T, T), 1)
    on_diag = rows == cols
    found = [jnp.where(on_diag, 1.0 / jnp.where(on_diag, b, 1.0), 0.0) for b in blocks]
    size = 1
    while size < T:
        below = (
            (rows // (2 * size) == cols // (2 * size))
            & ((rows // size) % 2 == 1)
            & ((cols // size) % 2 == 0)
        )
        offs = [jnp.where(below, b, 0.0) for b in blocks]
        mids = [product(left_form(o), right_form(x)) for o, x in zip(offs, found)]
        found = [x - product(left_form(x), right_form(m)) for x, m in zip(found, mids)]
        size *= 2
    return found


def relay_table(planes):
    windows = ((9.5, 21.0), (15.0, 21.0), (21.0, 33.0), (31.0, 43.0), (36.5, 43.0), (48.0, 55.0))
    starts = (6.4, 4.7, 2.2, 0.0, 7.4, 10.5, 14.1, 12.3)

    def reached(k, z):
        apart = (z - k) % planes
        return 14.4 + 5.4 * k + 3.1 * min(apart, planes - apart)

    table, first = [], [0] * planes
    for ready, limit in windows:
        steps = []
        for z in range(planes):
            there = ready + starts[z] + 3.0
            slack = 0.8 * (max(starts) - starts[z])

            def cost(k):
                when = reached(k, z)
                late = 0.3 * max(when - there, 0.0) + max(when - limit - starts[z] - slack, 0.0)
                if k < z - 1:
                    late += 6.0 * max(there + 1.0 - reached(z - 1, z), 0.0)
                return late + 0.3 * max(there - when, 0.0)

            steps.append(min(range(first[z], planes), key=cost))
        first = steps
        table.append(steps)
    return table


def kernel(
    d_hbm, z_hbm, a_hbm, norm_ref,
    norm_out, update_ref,
    panel, lower, zbuf, acc, solved, solved_right, inverse,
    own_sem, send_a, recv_a, send_l, recv_l, send_z, recv_z, send_s, recv_s, send_d,
):
    row = lax.axis_index("row")
    col = lax.axis_index("col")
    z, hi = row // 2, row % 2
    lo, x, core = col // 8, (col // 2) % 4, col % 2
    height = a_hbm.shape[0]
    piece_rows = height // PIECES
    planes = 8

    def place(lo_, x_, core_):
        return lo_ * 8 + x_ * 2 + core_

    x_next, x_prev, x_far = (x + 1) % 4, (x + 3) % 4, (x + 2) % 4
    to_x_next = {"row": row, "col": place(lo, x_next, core)}
    to_x_prev = {"row": row, "col": place(lo, x_prev, core)}
    to_y = {"row": row, "col": place(1 - lo, x, core)}
    to_sibling = {"row": row, "col": place(lo, x, 1 - core)}
    to_pair_l = {"row": z * 2 + 1 - hi, "col": place(1 - lo, x, core)}
    to_pair_z = {"row": z * 2 + 1 - hi, "col": col}
    to_z_next = {"row": ((z + 1) % planes) * 2 + hi, "col": col}
    to_z_prev = {"row": ((z + planes - 1) % planes) * 2 + hi, "col": col}
    partners = [to_x_next, to_x_prev, to_y, to_sibling, to_pair_l, to_pair_z, to_z_next, to_z_prev]

    own_copies = [pltpu.make_async_copy(a_hbm, panel.at[col], own_sem.at[0])]
    own_copies.append(pltpu.make_async_copy(z_hbm, zbuf.at[hi], own_sem.at[1]))
    for j in range(planes):
        own_copies.append(
            pltpu.make_async_copy(d_hbm.at[:, pl.ds(2 * T * j, 2 * T)], lower.at[hi, j], own_sem.at[2 + j])
        )
    for c in own_copies:
        c.start()

    barrier = pltpu.get_barrier_semaphore()
    for d in partners:
        pl.semaphore_signal(barrier, inc=1, device_id=d, device_id_type=pl.DeviceIdType.MESH)
    last = planes - 1
    opposite = 3

    @pl.when(z == opposite)
    def _():
        pl.semaphore_signal(
            barrier, inc=1, device_id={"row": 2 * last + hi, "col": col}, device_id_type=pl.DeviceIdType.MESH
        )

    pl.semaphore_wait(barrier, len(partners) + jnp.where(z == last, 1, 0))

    def remote(src, dst, s, r, target):
        return pltpu.make_async_remote_copy(
            src_ref=src, dst_ref=dst, send_sem=s, recv_sem=r,
            device_id=target, device_id_type=pl.DeviceIdType.MESH,
        )

    def lower_copy(j):
        return remote(
            d_hbm.at[:, pl.ds(2 * T * j, 2 * T)], lower.at[hi, j], send_l.at[j], recv_l.at[j], to_pair_l
        )

    def lower_arrived(j):
        remote(lower.at[1 - hi, j], lower.at[1 - hi, j], send_l.at[j], recv_l.at[j], to_pair_l).wait_recv()

    for j in range(planes):
        @pl.when(z == j)
        def _():
            lower_copy(j).start()
    z_copy = remote(z_hbm, zbuf.at[hi], send_z.at[0], recv_z.at[0], to_pair_z)
    z_copy.start()
    for j in range(planes):
        @pl.when(z > j)
        def _():
            lower_copy(j).start()

    pending = []

    def span(p):
        return pl.ds(p * piece_rows, piece_rows)

    def panel_copy(src, slot, p, index, target):
        return remote(src, panel.at[slot, span(p)], send_a.at[index], recv_a.at[slot, p], target)

    def send_own(p, target):
        panel_copy(a_hbm.at[span(p)], col, p, len(pending), target).start()
        pending.append((col, p, target))

    slots = {
        (side, where): place(side_lo, where_x, core)
        for side, side_lo in (("own", lo), ("other", 1 - lo))
        for where, where_x in (("here", x), ("prev", x_prev), ("next", x_next), ("far", x_far))
    }

    def wait_panel(slot, p):
        view = panel.at[slot, span(p)]
        remote(view, view, send_a.at[0], recv_a.at[slot, p], to_sibling).wait_recv()

    for p, q, y in zip((0, 2, 1, 3), (1, 3, 0, 2), (2, 3, 0, 1)):
        send_own(p, to_x_next)
        send_own(q, to_x_prev)
        send_own(y, to_y)
        send_own(p, to_sibling)

    prev, following, far = ("own", "prev"), ("own", "next"), ("own", "far")
    across, across_prev, across_next = ("other", "here"), ("other", "prev"), ("other", "next")
    every = range(PIECES)
    groups = [
        (
            [(prev, 0, to_x_next), (following, 1, to_x_prev), (across, 2, to_x_next),
             (prev, 0, to_y), (following, 1, to_y)],
            [], [("own", "here")],
        ),
        (
            [(across, 3, to_x_prev), (across, 2, to_x_prev), (across, 3, to_x_next),
             (prev, 2, to_x_next), (following, 3, to_x_prev)],
            [], [],
        ),
        ([(prev, 1, to_y), (following, 0, to_y)], [(across, 0)], []),
        ([(far, 0, to_y), (far, 1, to_y)], [(prev, 3), (following, 2), (across, 1)], []),
        (
            [(across_prev, 2, to_x_next), (across_next, 3, to_x_prev)],
            [(across_prev, 0), (across_next, 1)], [prev, following, across],
        ),
        (
            [], [(across_prev, 3), (across_next, 2), (across_prev, 1), (far, 2), (far, 3)],
            [far, across_prev],
        ),
        ([], [(("other", "far"), p) for p in (0, 2, 3, 1)] + [(across_next, 0)], [across_next, ("other", "far")]),
    ]
    plans = []
    arrived = set()
    for onward, taken, beside in groups:
        plan = []
        for key, p, target in onward + [(key, p, None) for key, p in taken]:
            if (key, p) not in arrived:
                arrived.add((key, p))
                plan.append((slots[key], p, None, None))
                plan.append((slots[key], p, len(pending), to_sibling))
                pending.append((slots[key], p, to_sibling))
            if target is not None:
                plan.append((slots[key], p, len(pending), target))
                pending.append((slots[key], p, target))
        plans.append((plan, beside))

    def relay(group):
        plan, beside = plans[group]
        for slot, p, index, target in plan:
            if target is None:
                wait_panel(slot, p)
            else:
                panel_copy(panel.at[slot, span(p)], slot, p, index, target).start()
        for key in beside:
            for p in every:
                wait_panel(slots[key] + 1 - 2 * core, p)

    relay_steps = relay_table(planes)

    def by_plane(values):
        picked = jnp.int32(values[0])
        for v in range(1, planes):
            picked = jnp.where(z == v, values[v], picked)
        return picked

    def relay_due(k):
        for group, steps in enumerate(relay_steps):
            here = [v for v in range(planes) if steps[v] == k]
            if len(here) == planes:
                relay(group)
            elif here:
                chosen = z == here[0]
                for v in here[1:]:
                    chosen = chosen | (z == v)

                @pl.when(chosen)
                def _():
                    relay(group)

    tile_rows = 512
    chip = lo * 4 + x

    def multiply(pair):
        right = solved_right[pl.ds(2 * pair, 2)].reshape(4 * T, 2 * T)

        for t in range(height // tile_rows):
            part = pl.ds(t * tile_rows, tile_rows)
            left = jnp.concatenate(
                [left_form(panel[2 * pair, part]), left_form(panel[2 * pair + 1, part])], axis=1
            )
            update_ref[part] += product(left, right)

    def step_of(pair):
        same_plane = pair // 4 == lo
        apart = (pair % 4 - x + 4) % 4
        near = jnp.where(same_plane, apart != 2, apart == 0)
        middle = jnp.where(same_plane, apart == 2, apart == 3)
        here = same_plane & (apart == 0)
        phase = jnp.where(middle, by_plane(relay_steps[5]), planes)
        phase = jnp.where(near, by_plane(relay_steps[4]), phase)
        phase = jnp.where(here, by_plane(relay_steps[0]), phase)
        due = jnp.maximum(pair, phase)
        return due

    def multiply_due(k):
        def one(pair, carry):
            @pl.when(step_of(pair) == k)
            def _():
                multiply(pair)

            return carry

        lax.fori_loop(0, planes, one, 0)

    for c in own_copies:
        c.wait()
    z_copy.wait_send()
    remote(zbuf.at[1 - hi], zbuf.at[1 - hi], send_z.at[0], recv_z.at[0], to_pair_z).wait_recv()
    for j in range(planes):
        @pl.when(z == j)
        def _():
            lower_arrived(j)
    acc[...] = zbuf[...].reshape(2 * T, T)
    update_ref[...] = jnp.zeros_like(update_ref)
    first_rows = lower[0, z]
    second_rows = lower[1, z]
    inv_a, inv_b = invert_lower([first_rows[:, :T], second_rows[:, T:]])
    inverse[0] = left_form(inv_a)
    inverse[1] = left_form(inv_b)
    inverse[2] = left_form(second_rows[:, :T])

    def solved_copy(k, half, target, way):
        view = solved.at[2 * k + half]
        return remote(view, view, send_s.at[way, 2 * k + half], recv_s.at[2 * k + half], target)

    def direct_copy(half):
        view = solved.at[2 * last + half]
        target = {"row": 2 * opposite + hi, "col": col}
        return remote(view, view, send_d.at[half], recv_s.at[2 * last + half], target)

    def spread(k, half):
        dist = (z - k + planes) % planes

        @pl.when(dist <= (3 if k < last else 2))
        def _():
            solved_copy(k, half, to_z_next, 0).start()

        @pl.when((dist == 0) | (dist >= 6))
        def _():
            solved_copy(k, half, to_z_prev, 1).start()

        if k == last and half == 1:
            @pl.when(dist == 0)
            def _():
                direct_copy(0).start()
                direct_copy(1).start()

    def solve_own(k, rest_a, rest_b):
        s_a = product(inverse[0], right_form(rest_a))
        solved[2 * k] = s_a
        spread(k, 0)
        solved[2 * k + 1] = product(inverse[1], right_form(rest_b() - product(inverse[2], right_form(s_a))))
        spread(k, 1)

    @pl.when(z == 0)
    def _():
        solve_own(0, acc[:T], lambda: acc[T:])

    for k in range(planes):
        @pl.when(z > k)
        def _():
            lower_arrived(k)
            tile = lower[:, k].reshape(2 * T, 2 * T)
            solved_copy(k, 0, to_z_next, 0).wait_recv()
            spread(k, 0)
            acc[...] -= product(left_form(tile[:, :T]), right_form(solved[2 * k]))
            solved_copy(k, 1, to_z_next, 0).wait_recv()
            spread(k, 1)
            right = right_form(solved[2 * k + 1])

            @pl.when(z == k + 1)
            def _():
                if k + 1 < planes:
                    solve_own(
                        k + 1,
                        acc[:T] - product(left_form(tile[:T, T:]), right),
                        lambda: acc[T:] - product(left_form(tile[T:, T:]), right),
                    )

            @pl.when(z > k + 1)
            def _():
                acc[...] -= product(left_form(tile[:, T:]), right)

        @pl.when(z < k)
        def _():
            for half in range(2):
                solved_copy(k, half, to_z_next, 0).wait_recv()
                spread(k, half)

        for half in range(2):
            solved_right[2 * k + half] = right_form(solved[2 * k + half])
        relay_due(k)
        multiply_due(k)

    relay(len(groups) - 1)
    multiply_due(planes)
    total = norm_ref[...]
    for k in range(2 * planes):
        block = solved[k]
        total = total + jnp.sum(block * block, axis=0, keepdims=True)
    norm_out[...] = total

    for index, (slot, p, target) in enumerate(pending):
        panel_copy(panel.at[slot, span(p)], slot, p, index, target).wait_send()
    for j in range(planes):
        @pl.when(z >= j)
        def _():
            lower_copy(j).wait_send()
    for k in range(planes):
        dist = (z - k + planes) % planes
        for half in range(2):
            @pl.when(dist <= (3 if k < last else 2))
            def _():
                solved_copy(k, half, to_z_next, 0).wait_send()

            if k == last:
                @pl.when(dist == 0)
                def _():
                    direct_copy(half).wait_send()

            @pl.when((dist == 0) | (dist >= 6))
            def _():
                solved_copy(k, half, to_z_prev, 1).wait_send()


def shards(diag_block, z_panel, panel_below, z_trail, norm_sq):
    height = panel_below.shape[0]
    dma = pltpu.SemaphoreType.DMA
    norm_out, update = pl.pallas_call(
        kernel,
        out_shape=(
            jax.ShapeDtypeStruct((1, T), F32),
            jax.ShapeDtypeStruct((height, T), F32),
        ),
        in_specs=[pl.BlockSpec(memory_space=pl.ANY)] * 3 + [pl.BlockSpec(memory_space=pltpu.VMEM)],
        out_specs=(pl.BlockSpec(memory_space=pltpu.VMEM),) * 2,
        scratch_shapes=[
            pltpu.VMEM((16, height, T), F32),
            pltpu.VMEM((2, 8, T, 2 * T), F32),
            pltpu.VMEM((2, T, T), F32),
            pltpu.VMEM((2 * T, T), F32),
            pltpu.VMEM((16, T, T), F32),
            pltpu.VMEM((16, 2 * T, 2 * T), BF16),
            pltpu.VMEM((3, T, 2 * T), BF16),
            dma((10,)), dma((64,)), dma((16, PIECES)), dma((8,)), dma((8,)),
            dma((1,)), dma((1,)), dma((2, 16)), dma((16,)), dma((2,)),
        ],
        compiler_params=pltpu.CompilerParams(
            collective_id=0, has_side_effects=True, vmem_limit_bytes=67_043_328
        ),
        name="panel_update",
    )(diag_block, z_panel, panel_below, norm_sq.reshape(1, T))
    return norm_out.reshape(T), z_trail - update


def solution(mesh):
    return jax.shard_map(
        shards,
        mesh=mesh,
        in_specs=(P("row", None), P("row", "col"), P("row", "col"), P("row", "col"), P("col")),
        out_specs=(P("col"), P("row", "col")),
        check_vma=False,
    )
```

```python
import jax
import jax.numpy as jnp
from jax import lax
from jax.experimental import pallas as pl
from jax.experimental.pallas import tpu as pltpu
from jax.sharding import PartitionSpec as P

F32 = jnp.float32
BF16 = jnp.bfloat16
T = 128
PIECES = 4


def halves(v):
    high = v.astype(BF16)
    low = (v - high.astype(F32)).astype(BF16)
    return high, low


def left_form(v):
    high, low = halves(v)
    return jnp.concatenate([high, low], axis=1)


def right_form(v):
    high, low = halves(v)
    both = jnp.concatenate([high, low], axis=1)
    return jnp.concatenate([both, both], axis=0)


def product(left, right):
    wide = jnp.dot(left, right, preferred_element_type=F32)
    return wide[:, :T] + wide[:, T:]


def invert_lower(blocks):
    rows = lax.broadcasted_iota(jnp.int32, (T, T), 0)
    cols = lax.broadcasted_iota(jnp.int32, (T, T), 1)
    on_diag = rows == cols
    found = [jnp.where(on_diag, 1.0 / jnp.where(on_diag, b, 1.0), 0.0) for b in blocks]
    size = 1
    while size < T:
        below = (
            (rows // (2 * size) == cols // (2 * size))
            & ((rows // size) % 2 == 1)
            & ((cols // size) % 2 == 0)
        )
        offs = [jnp.where(below, b, 0.0) for b in blocks]
        mids = [product(left_form(o), right_form(x)) for o, x in zip(offs, found)]
        found = [x - product(left_form(x), right_form(m)) for x, m in zip(found, mids)]
        size *= 2
    return found


def relay_table(planes):
    windows = ((9.5, 21.0), (15.0, 21.0), (21.0, 33.0), (31.0, 43.0), (36.5, 43.0), (48.0, 55.0))
    starts = (6.4, 4.7, 2.2, 0.0, 7.4, 10.5, 14.1, 12.3)

    def reached(k, z):
        apart = (z - k) % planes
        return 14.4 + 5.4 * k + 3.1 * min(apart, planes - apart)

    table, first = [], [0] * planes
    for ready, limit in windows:
        steps = []
        for z in range(planes):
            there = ready + starts[z] + 3.0
            slack = 0.8 * (max(starts) - starts[z])

            def cost(k):
                when = reached(k, z)
                late = 0.3 * max(when - there, 0.0) + max(when - limit - starts[z] - slack, 0.0)
                if k < z - 1:
                    late += 6.0 * max(there + 1.0 - reached(z - 1, z), 0.0)
                return late + 0.3 * max(there - when, 0.0)

            steps.append(min(range(first[z], planes), key=cost))
        first = steps
        table.append(steps)
    return table


def kernel(
    d_hbm, z_hbm, a_hbm, norm_ref,
    norm_out, update_ref,
    panel, lower, zbuf, acc, solved, solved_right, inverse,
    own_sem, send_a, recv_a, send_l, recv_l, send_z, recv_z, send_s, recv_s, send_d,
):
    row = lax.axis_index("row")
    col = lax.axis_index("col")
    z, hi = row // 2, row % 2
    lo, x, core = col // 8, (col // 2) % 4, col % 2
    height = a_hbm.shape[0]
    piece_rows = height // PIECES
    planes = 8

    def place(lo_, x_, core_):
        return lo_ * 8 + x_ * 2 + core_

    x_next, x_prev, x_far = (x + 1) % 4, (x + 3) % 4, (x + 2) % 4
    to_x_next = {"row": row, "col": place(lo, x_next, core)}
    to_x_prev = {"row": row, "col": place(lo, x_prev, core)}
    to_y = {"row": row, "col": place(1 - lo, x, core)}
    to_sibling = {"row": row, "col": place(lo, x, 1 - core)}
    to_pair_l = {"row": z * 2 + 1 - hi, "col": place(1 - lo, x, core)}
    to_pair_z = {"row": z * 2 + 1 - hi, "col": col}
    to_z_next = {"row": ((z + 1) % planes) * 2 + hi, "col": col}
    to_z_prev = {"row": ((z + planes - 1) % planes) * 2 + hi, "col": col}
    partners = [to_x_next, to_x_prev, to_y, to_sibling, to_pair_l, to_pair_z, to_z_next, to_z_prev]

    own_copies = [pltpu.make_async_copy(a_hbm, panel.at[col], own_sem.at[0])]
    own_copies.append(pltpu.make_async_copy(z_hbm, zbuf.at[hi], own_sem.at[1]))
    for j in range(planes):
        own_copies.append(
            pltpu.make_async_copy(d_hbm.at[:, pl.ds(2 * T * j, 2 * T)], lower.at[hi, j], own_sem.at[2 + j])
        )
    for c in own_copies:
        c.start()

    barrier = pltpu.get_barrier_semaphore()
    for d in partners:
        pl.semaphore_signal(barrier, inc=1, device_id=d, device_id_type=pl.DeviceIdType.MESH)
    last = planes - 1
    opposite = 3

    @pl.when(z == opposite)
    def _():
        pl.semaphore_signal(
            barrier, inc=1, device_id={"row": 2 * last + hi, "col": col}, device_id_type=pl.DeviceIdType.MESH
        )

    pl.semaphore_wait(barrier, len(partners) + jnp.where(z == last, 1, 0))

    def remote(src, dst, s, r, target):
        return pltpu.make_async_remote_copy(
            src_ref=src, dst_ref=dst, send_sem=s, recv_sem=r,
            device_id=target, device_id_type=pl.DeviceIdType.MESH,
        )

    def lower_copy(j):
        return remote(
            d_hbm.at[:, pl.ds(2 * T * j, 2 * T)], lower.at[hi, j], send_l.at[j], recv_l.at[j], to_pair_l
        )

    def lower_arrived(j):
        remote(lower.at[1 - hi, j], lower.at[1 - hi, j], send_l.at[j], recv_l.at[j], to_pair_l).wait_recv()

    for j in range(planes):
        @pl.when(z == j)
        def _():
            lower_copy(j).start()
    z_copy = remote(z_hbm, zbuf.at[hi], send_z.at[0], recv_z.at[0], to_pair_z)
    z_copy.start()
    for j in range(planes):
        @pl.when(z > j)
        def _():
            lower_copy(j).start()

    pending = []

    def span(p):
        return pl.ds(p * piece_rows, piece_rows)

    def panel_copy(src, slot, p, index, target):
        return remote(src, panel.at[slot, span(p)], send_a.at[index], recv_a.at[slot, p], target)

    def send_own(p, target):
        panel_copy(a_hbm.at[span(p)], col, p, len(pending), target).start()
        pending.append((col, p, target))

    slots = {
        (side, where): place(side_lo, where_x, core)
        for side, side_lo in (("own", lo), ("other", 1 - lo))
        for where, where_x in (("here", x), ("prev", x_prev), ("next", x_next), ("far", x_far))
    }

    def wait_panel(slot, p):
        view = panel.at[slot, span(p)]
        remote(view, view, send_a.at[0], recv_a.at[slot, p], to_sibling).wait_recv()

    for p, q, y in zip((0, 2, 1, 3), (1, 3, 0, 2), (2, 3, 0, 1)):
        send_own(p, to_x_next)
        send_own(q, to_x_prev)
        send_own(y, to_y)
        send_own(p, to_sibling)

    prev, following, far = ("own", "prev"), ("own", "next"), ("own", "far")
    across, across_prev, across_next = ("other", "here"), ("other", "prev"), ("other", "next")
    every = range(PIECES)
    groups = [
        (
            [(prev, 0, to_x_next), (following, 1, to_x_prev), (across, 2, to_x_next),
             (prev, 0, to_y), (following, 1, to_y)],
            [], [("own", "here")],
        ),
        (
            [(across, 3, to_x_prev), (across, 2, to_x_prev), (across, 3, to_x_next),
             (prev, 2, to_x_next), (following, 3, to_x_prev)],
            [], [],
        ),
        ([(prev, 1, to_y), (following, 0, to_y)], [(across, 0)], []),
        ([(far, 0, to_y), (far, 1, to_y)], [(prev, 3), (following, 2), (across, 1)], []),
        (
            [(across_prev, 2, to_x_next), (across_next, 3, to_x_prev)],
            [(across_prev, 0), (across_next, 1)], [prev, following, across],
        ),
        (
            [], [(across_prev, 3), (across_next, 2), (across_prev, 1), (far, 2), (far, 3)],
            [far, across_prev],
        ),
        ([], [(("other", "far"), p) for p in (0, 2, 3, 1)] + [(across_next, 0)], [across_next, ("other", "far")]),
    ]
    plans = []
    arrived = set()
    for onward, taken, beside in groups:
        plan = []
        for key, p, target in onward + [(key, p, None) for key, p in taken]:
            if (key, p) not in arrived:
                arrived.add((key, p))
                plan.append((slots[key], p, None, None))
                plan.append((slots[key], p, len(pending), to_sibling))
                pending.append((slots[key], p, to_sibling))
            if target is not None:
                plan.append((slots[key], p, len(pending), target))
                pending.append((slots[key], p, target))
        plans.append((plan, beside))

    def relay(group):
        plan, beside = plans[group]
        for slot, p, index, target in plan:
            if target is None:
                wait_panel(slot, p)
            else:
                panel_copy(panel.at[slot, span(p)], slot, p, index, target).start()
        for key in beside:
            for p in every:
                wait_panel(slots[key] + 1 - 2 * core, p)

    relay_steps = relay_table(planes)

    def by_plane(values):
        picked = jnp.int32(values[0])
        for v in range(1, planes):
            picked = jnp.where(z == v, values[v], picked)
        return picked

    def relay_due(k):
        for group, steps in enumerate(relay_steps):
            here = [v for v in range(planes) if steps[v] == k]
            if len(here) == planes:
                relay(group)
            elif here:
                chosen = z == here[0]
                for v in here[1:]:
                    chosen = chosen | (z == v)

                @pl.when(chosen)
                def _():
                    relay(group)

    tile_rows = 512
    chip = lo * 4 + x

    def multiply(pair):
        right = solved_right[pl.ds(2 * pair, 2)].reshape(4 * T, 2 * T)

        for t in range(height // tile_rows):
            part = pl.ds(t * tile_rows, tile_rows)
            left = jnp.concatenate(
                [left_form(panel[2 * pair, part]), left_form(panel[2 * pair + 1, part])], axis=1
            )
            update_ref[part] += product(left, right)

    def step_of(pair):
        same_plane = pair // 4 == lo
        apart = (pair % 4 - x + 4) % 4
        near = jnp.where(same_plane, apart != 2, apart == 0)
        middle = jnp.where(same_plane, apart == 2, apart == 3)
        here = same_plane & (apart == 0)
        phase = jnp.where(middle, by_plane(relay_steps[5]), planes)
        phase = jnp.where(near, by_plane(relay_steps[4]), phase)
        phase = jnp.where(here, by_plane(relay_steps[0]), phase)
        due = jnp.maximum(pair, phase)
        return due

    def multiply_due(k):
        def one(pair, carry):
            @pl.when(step_of(pair) == k)
            def _():
                multiply(pair)

            return carry

        lax.fori_loop(0, planes, one, 0)

    for c in own_copies:
        c.wait()
    z_copy.wait_send()
    remote(zbuf.at[1 - hi], zbuf.at[1 - hi], send_z.at[0], recv_z.at[0], to_pair_z).wait_recv()
    for j in range(planes):
        @pl.when(z == j)
        def _():
            lower_arrived(j)
    acc[...] = zbuf[...].reshape(2 * T, T)
    update_ref[...] = jnp.zeros_like(update_ref)
    first_rows = lower[0, z]
    second_rows = lower[1, z]
    inv_a, inv_b = invert_lower([first_rows[:, :T], second_rows[:, T:]])
    inverse[0] = left_form(inv_a)
    inverse[1] = left_form(inv_b)
    inverse[2] = left_form(second_rows[:, :T])

    def solved_copy(k, half, target, way):
        view = solved.at[2 * k + half]
        return remote(view, view, send_s.at[way, 2 * k + half], recv_s.at[2 * k + half], target)

    def direct_copy(half):
        view = solved.at[2 * last + half]
        target = {"row": 2 * opposite + hi, "col": col}
        return remote(view, view, send_d.at[half], recv_s.at[2 * last + half], target)

    def spread(k, half):
        dist = (z - k + planes) % planes

        @pl.when(dist <= (3 if k < last else 1))
        def _():
            solved_copy(k, half, to_z_next, 0).start()

        @pl.when((dist == 0) | (dist >= 6) | (dist == (4 if k == last else 0)))
        def _():
            solved_copy(k, half, to_z_prev, 1).start()

        if k == last and half == 1:
            @pl.when(dist == 0)
            def _():
                direct_copy(0).start()
                direct_copy(1).start()

    def solve_own(k, rest_a, rest_b):
        s_a = product(inverse[0], right_form(rest_a))
        solved[2 * k] = s_a
        spread(k, 0)
        solved[2 * k + 1] = product(inverse[1], right_form(rest_b() - product(inverse[2], right_form(s_a))))
        spread(k, 1)

    @pl.when(z == 0)
    def _():
        solve_own(0, acc[:T], lambda: acc[T:])

    for k in range(planes):
        @pl.when(z > k)
        def _():
            lower_arrived(k)
            tile = lower[:, k].reshape(2 * T, 2 * T)
            solved_copy(k, 0, to_z_next, 0).wait_recv()
            spread(k, 0)
            acc[...] -= product(left_form(tile[:, :T]), right_form(solved[2 * k]))
            solved_copy(k, 1, to_z_next, 0).wait_recv()
            spread(k, 1)
            right = right_form(solved[2 * k + 1])

            @pl.when(z == k + 1)
            def _():
                if k + 1 < planes:
                    solve_own(
                        k + 1,
                        acc[:T] - product(left_form(tile[:T, T:]), right),
                        lambda: acc[T:] - product(left_form(tile[T:, T:]), right),
                    )

            @pl.when(z > k + 1)
            def _():
                acc[...] -= product(left_form(tile[:, T:]), right)

        @pl.when(z < k)
        def _():
            for half in range(2):
                solved_copy(k, half, to_z_next, 0).wait_recv()
                spread(k, half)

        for half in range(2):
            solved_right[2 * k + half] = right_form(solved[2 * k + half])
        relay_due(k)
        multiply_due(k)

    relay(len(groups) - 1)
    multiply_due(planes)
    total = norm_ref[...]
    for k in range(2 * planes):
        block = solved[k]
        total = total + jnp.sum(block * block, axis=0, keepdims=True)
    norm_out[...] = total

    for index, (slot, p, target) in enumerate(pending):
        panel_copy(panel.at[slot, span(p)], slot, p, index, target).wait_send()
    for j in range(planes):
        @pl.when(z >= j)
        def _():
            lower_copy(j).wait_send()
    for k in range(planes):
        dist = (z - k + planes) % planes
        for half in range(2):
            @pl.when(dist <= (3 if k < last else 1))
            def _():
                solved_copy(k, half, to_z_next, 0).wait_send()

            if k == last:
                @pl.when(dist == 0)
                def _():
                    direct_copy(half).wait_send()

            @pl.when((dist == 0) | (dist >= 6) | (dist == (4 if k == last else 0)))
            def _():
                solved_copy(k, half, to_z_prev, 1).wait_send()


def shards(diag_block, z_panel, panel_below, z_trail, norm_sq):
    height = panel_below.shape[0]
    dma = pltpu.SemaphoreType.DMA
    norm_out, update = pl.pallas_call(
        kernel,
        out_shape=(
            jax.ShapeDtypeStruct((1, T), F32),
            jax.ShapeDtypeStruct((height, T), F32),
        ),
        in_specs=[pl.BlockSpec(memory_space=pl.ANY)] * 3 + [pl.BlockSpec(memory_space=pltpu.VMEM)],
        out_specs=(pl.BlockSpec(memory_space=pltpu.VMEM),) * 2,
        scratch_shapes=[
            pltpu.VMEM((16, height, T), F32),
            pltpu.VMEM((2, 8, T, 2 * T), F32),
            pltpu.VMEM((2, T, T), F32),
            pltpu.VMEM((2 * T, T), F32),
            pltpu.VMEM((16, T, T), F32),
            pltpu.VMEM((16, 2 * T, 2 * T), BF16),
            pltpu.VMEM((3, T, 2 * T), BF16),
            dma((10,)), dma((64,)), dma((16, PIECES)), dma((8,)), dma((8,)),
            dma((1,)), dma((1,)), dma((2, 16)), dma((16,)), dma((2,)),
        ],
        compiler_params=pltpu.CompilerParams(
            collective_id=0, has_side_effects=True, vmem_limit_bytes=67_043_328
        ),
        name="panel_update",
    )(diag_block, z_panel, panel_below, norm_sq.reshape(1, T))
    return norm_out.reshape(T), z_trail - update


def solution(mesh):
    return jax.shard_map(
        shards,
        mesh=mesh,
        in_specs=(P("row", None), P("row", "col"), P("row", "col"), P("row", "col"), P("col")),
        out_specs=(P("col"), P("row", "col")),
        check_vma=False,
    )
```

```python
import jax
import jax.numpy as jnp
from jax import lax
from jax.experimental import pallas as pl
from jax.experimental.pallas import tpu as pltpu
from jax.sharding import PartitionSpec as P

F32 = jnp.float32
BF16 = jnp.bfloat16
T = 128
PIECES = 4


def halves(v):
    high = v.astype(BF16)
    low = (v - high.astype(F32)).astype(BF16)
    return high, low


def left_form(v):
    high, low = halves(v)
    return jnp.concatenate([high, low], axis=1)


def right_form(v):
    high, low = halves(v)
    both = jnp.concatenate([high, low], axis=1)
    return jnp.concatenate([both, both], axis=0)


def product(left, right):
    wide = jnp.dot(left, right, preferred_element_type=F32)
    return wide[:, :T] + wide[:, T:]


def invert_lower(blocks):
    rows = lax.broadcasted_iota(jnp.int32, (T, T), 0)
    cols = lax.broadcasted_iota(jnp.int32, (T, T), 1)
    on_diag = rows == cols
    found = [jnp.where(on_diag, 1.0 / jnp.where(on_diag, b, 1.0), 0.0) for b in blocks]
    size = 1
    while size < T:
        below = (
            (rows // (2 * size) == cols // (2 * size))
            & ((rows // size) % 2 == 1)
            & ((cols // size) % 2 == 0)
        )
        offs = [jnp.where(below, b, 0.0) for b in blocks]
        mids = [product(left_form(o), right_form(x)) for o, x in zip(offs, found)]
        found = [x - product(left_form(x), right_form(m)) for x, m in zip(found, mids)]
        size *= 2
    return found


def relay_table(planes):
    windows = ((9.5, 21.0), (15.0, 21.0), (21.0, 33.0), (31.0, 43.0), (36.5, 43.0), (48.0, 55.0))
    starts = (6.4, 4.7, 2.2, 0.0, 7.4, 10.5, 14.1, 12.3)

    def reached(k, z):
        apart = (z - k) % planes
        return 14.4 + 5.4 * k + 3.1 * min(apart, planes - apart)

    table, first = [], [0] * planes
    for ready, limit in windows:
        steps = []
        for z in range(planes):
            there = ready + starts[z] + 3.0
            slack = 0.8 * (max(starts) - starts[z])

            def cost(k):
                when = reached(k, z)
                late = 0.3 * max(when - there, 0.0) + max(when - limit - starts[z] - slack, 0.0)
                if k < z - 1:
                    late += 6.0 * max(there + 1.0 - reached(z - 1, z), 0.0)
                return late + 0.3 * max(there - when, 0.0)

            steps.append(min(range(first[z], planes), key=cost))
        first = steps
        table.append(steps)
    return table


def kernel(
    d_hbm, z_hbm, a_hbm, norm_ref,
    norm_out, update_ref,
    panel, lower, zbuf, acc, solved, solved_right, inverse,
    own_sem, send_a, recv_a, send_l, recv_l, send_z, recv_z, send_s, recv_s, send_d,
):
    row = lax.axis_index("row")
    col = lax.axis_index("col")
    z, hi = row // 2, row % 2
    lo, x, core = col // 8, (col // 2) % 4, col % 2
    height = a_hbm.shape[0]
    piece_rows = height // PIECES
    planes = 8

    def place(lo_, x_, core_):
        return lo_ * 8 + x_ * 2 + core_

    x_next, x_prev, x_far = (x + 1) % 4, (x + 3) % 4, (x + 2) % 4
    to_x_next = {"row": row, "col": place(lo, x_next, core)}
    to_x_prev = {"row": row, "col": place(lo, x_prev, core)}
    to_y = {"row": row, "col": place(1 - lo, x, core)}
    to_sibling = {"row": row, "col": place(lo, x, 1 - core)}
    to_pair_l = {"row": z * 2 + 1 - hi, "col": place(1 - lo, x, core)}
    to_pair_z = {"row": z * 2 + 1 - hi, "col": col}
    to_z_next = {"row": ((z + 1) % planes) * 2 + hi, "col": col}
    to_z_prev = {"row": ((z + planes - 1) % planes) * 2 + hi, "col": col}
    partners = [to_x_next, to_x_prev, to_y, to_sibling, to_pair_l, to_pair_z, to_z_next, to_z_prev]

    own_copies = [pltpu.make_async_copy(a_hbm, panel.at[col], own_sem.at[0])]
    own_copies.append(pltpu.make_async_copy(z_hbm, zbuf.at[hi], own_sem.at[1]))
    for j in range(planes):
        own_copies.append(
            pltpu.make_async_copy(d_hbm.at[:, pl.ds(2 * T * j, 2 * T)], lower.at[hi, j], own_sem.at[2 + j])
        )
    for c in own_copies:
        c.start()

    barrier = pltpu.get_barrier_semaphore()
    for d in partners:
        pl.semaphore_signal(barrier, inc=1, device_id=d, device_id_type=pl.DeviceIdType.MESH)
    last = planes - 1
    opposite = 3

    @pl.when(z == opposite)
    def _():
        pl.semaphore_signal(
            barrier, inc=1, device_id={"row": 2 * last + hi, "col": col}, device_id_type=pl.DeviceIdType.MESH
        )

    pl.semaphore_wait(barrier, len(partners) + jnp.where(z == last, 1, 0))

    def remote(src, dst, s, r, target):
        return pltpu.make_async_remote_copy(
            src_ref=src, dst_ref=dst, send_sem=s, recv_sem=r,
            device_id=target, device_id_type=pl.DeviceIdType.MESH,
        )

    def lower_copy(j):
        return remote(
            d_hbm.at[:, pl.ds(2 * T * j, 2 * T)], lower.at[hi, j], send_l.at[j], recv_l.at[j], to_pair_l
        )

    def lower_arrived(j):
        remote(lower.at[1 - hi, j], lower.at[1 - hi, j], send_l.at[j], recv_l.at[j], to_pair_l).wait_recv()

    for j in range(planes):
        @pl.when(z == j)
        def _():
            lower_copy(j).start()
    z_copy = remote(z_hbm, zbuf.at[hi], send_z.at[0], recv_z.at[0], to_pair_z)
    z_copy.start()
    for j in range(planes):
        @pl.when(z > j)
        def _():
            lower_copy(j).start()

    pending = []

    def span(p):
        return pl.ds(p * piece_rows, piece_rows)

    def panel_copy(src, slot, p, index, target):
        return remote(src, panel.at[slot, span(p)], send_a.at[index], recv_a.at[slot, p], target)

    def send_own(p, target):
        panel_copy(a_hbm.at[span(p)], col, p, len(pending), target).start()
        pending.append((col, p, target))

    slots = {
        (side, where): place(side_lo, where_x, core)
        for side, side_lo in (("own", lo), ("other", 1 - lo))
        for where, where_x in (("here", x), ("prev", x_prev), ("next", x_next), ("far", x_far))
    }

    def wait_panel(slot, p):
        view = panel.at[slot, span(p)]
        remote(view, view, send_a.at[0], recv_a.at[slot, p], to_sibling).wait_recv()

    for p, q, y in zip((0, 2, 1, 3), (1, 3, 0, 2), (2, 3, 0, 1)):
        send_own(p, to_x_next)
        send_own(q, to_x_prev)
        send_own(y, to_y)
        send_own(p, to_sibling)

    prev, following, far = ("own", "prev"), ("own", "next"), ("own", "far")
    across, across_prev, across_next = ("other", "here"), ("other", "prev"), ("other", "next")
    every = range(PIECES)
    groups = [
        (
            [(prev, 0, to_x_next), (following, 1, to_x_prev), (across, 2, to_x_next),
             (prev, 0, to_y), (following, 1, to_y)],
            [], [("own", "here")],
        ),
        (
            [(across, 3, to_x_prev), (across, 2, to_x_prev), (across, 3, to_x_next),
             (prev, 2, to_x_next), (following, 3, to_x_prev)],
            [], [],
        ),
        ([(prev, 1, to_y), (following, 0, to_y)], [(across, 0)], []),
        ([(far, 0, to_y), (far, 1, to_y)], [(prev, 3), (following, 2), (across, 1)], []),
        (
            [(across_prev, 2, to_x_next), (across_next, 3, to_x_prev)],
            [(across_prev, 0), (across_next, 1)], [prev, following, across],
        ),
        (
            [], [(across_prev, 3), (across_next, 2), (across_prev, 1), (far, 2), (far, 3)],
            [far, across_prev],
        ),
        ([], [(("other", "far"), p) for p in (0, 2, 3, 1)] + [(across_next, 0)], [across_next, ("other", "far")]),
    ]
    plans = []
    arrived = set()
    for onward, taken, beside in groups:
        plan = []
        for key, p, target in onward + [(key, p, None) for key, p in taken]:
            if (key, p) not in arrived:
                arrived.add((key, p))
                plan.append((slots[key], p, None, None))
                plan.append((slots[key], p, len(pending), to_sibling))
                pending.append((slots[key], p, to_sibling))
            if target is not None:
                plan.append((slots[key], p, len(pending), target))
                pending.append((slots[key], p, target))
        plans.append((plan, beside))

    def relay(group):
        plan, beside = plans[group]
        for slot, p, index, target in plan:
            if target is None:
                wait_panel(slot, p)
            else:
                panel_copy(panel.at[slot, span(p)], slot, p, index, target).start()
        for key in beside:
            for p in every:
                wait_panel(slots[key] + 1 - 2 * core, p)

    relay_steps = relay_table(planes)

    def by_plane(values):
        picked = jnp.int32(values[0])
        for v in range(1, planes):
            picked = jnp.where(z == v, values[v], picked)
        return picked

    def relay_due(k):
        for group, steps in enumerate(relay_steps):
            here = [v for v in range(planes) if steps[v] == k]
            if len(here) == planes:
                relay(group)
            elif here:
                chosen = z == here[0]
                for v in here[1:]:
                    chosen = chosen | (z == v)

                @pl.when(chosen)
                def _():
                    relay(group)

    tile_rows = 512
    chip = lo * 4 + x

    def multiply(pair):
        right = solved_right[pl.ds(2 * pair, 2)].reshape(4 * T, 2 * T)

        for t in range(height // tile_rows):
            part = pl.ds(t * tile_rows, tile_rows)
            left = jnp.concatenate(
                [left_form(panel[2 * pair, part]), left_form(panel[2 * pair + 1, part])], axis=1
            )
            update_ref[part] += product(left, right)

    def step_of(pair):
        same_plane = pair // 4 == lo
        apart = (pair % 4 - x + 4) % 4
        near = jnp.where(same_plane, apart != 2, apart == 0)
        middle = jnp.where(same_plane, apart == 2, apart == 3)
        here = same_plane & (apart == 0)
        phase = jnp.where(middle, by_plane(relay_steps[5]), planes)
        phase = jnp.where(near, by_plane(relay_steps[4]), phase)
        phase = jnp.where(here, by_plane(relay_steps[0]), phase)
        due = jnp.maximum(pair, phase)
        return due

    def multiply_due(k):
        def one(pair, carry):
            @pl.when(step_of(pair) == k)
            def _():
                multiply(pair)

            return carry

        lax.fori_loop(0, planes, one, 0)

    for c in own_copies:
        c.wait()
    z_copy.wait_send()
    remote(zbuf.at[1 - hi], zbuf.at[1 - hi], send_z.at[0], recv_z.at[0], to_pair_z).wait_recv()
    for j in range(planes):
        @pl.when(z == j)
        def _():
            lower_arrived(j)
    acc[...] = zbuf[...].reshape(2 * T, T)
    update_ref[...] = jnp.zeros_like(update_ref)
    first_rows = lower[0, z]
    second_rows = lower[1, z]
    inv_a, inv_b = invert_lower([first_rows[:, :T], second_rows[:, T:]])
    inverse[0] = left_form(inv_a)
    inverse[1] = left_form(inv_b)
    inverse[2] = left_form(second_rows[:, :T])

    def solved_copy(k, half, target, way):
        view = solved.at[2 * k + half]
        return remote(view, view, send_s.at[way, 2 * k + half], recv_s.at[2 * k + half], target)

    def direct_copy(half):
        view = solved.at[2 * last + half]
        target = {"row": 2 * opposite + hi, "col": col}
        return remote(view, view, send_d.at[half], recv_s.at[2 * last + half], target)

    def spread(k, half):
        dist = (z - k + planes) % planes

        @pl.when(dist <= (3 if k < last else 0))
        def _():
            solved_copy(k, half, to_z_next, 0).start()

        @pl.when((dist == 0) | (dist >= 6) | ((dist == 3) | (dist == 4) if k == last else dist == 0))
        def _():
            solved_copy(k, half, to_z_prev, 1).start()

        if k == last and half == 1:
            @pl.when(dist == 0)
            def _():
                direct_copy(0).start()
                direct_copy(1).start()

    def solve_own(k, rest_a, rest_b):
        s_a = product(inverse[0], right_form(rest_a))
        solved[2 * k] = s_a
        spread(k, 0)
        solved[2 * k + 1] = product(inverse[1], right_form(rest_b() - product(inverse[2], right_form(s_a))))
        spread(k, 1)

    @pl.when(z == 0)
    def _():
        solve_own(0, acc[:T], lambda: acc[T:])

    for k in range(planes):
        @pl.when(z > k)
        def _():
            lower_arrived(k)
            tile = lower[:, k].reshape(2 * T, 2 * T)
            solved_copy(k, 0, to_z_next, 0).wait_recv()
            spread(k, 0)
            acc[...] -= product(left_form(tile[:, :T]), right_form(solved[2 * k]))
            solved_copy(k, 1, to_z_next, 0).wait_recv()
            spread(k, 1)
            right = right_form(solved[2 * k + 1])

            @pl.when(z == k + 1)
            def _():
                if k + 1 < planes:
                    solve_own(
                        k + 1,
                        acc[:T] - product(left_form(tile[:T, T:]), right),
                        lambda: acc[T:] - product(left_form(tile[T:, T:]), right),
                    )

            @pl.when(z > k + 1)
            def _():
                acc[...] -= product(left_form(tile[:, T:]), right)

        @pl.when(z < k)
        def _():
            for half in range(2):
                solved_copy(k, half, to_z_next, 0).wait_recv()
                spread(k, half)

        for half in range(2):
            solved_right[2 * k + half] = right_form(solved[2 * k + half])
        relay_due(k)
        multiply_due(k)

    relay(len(groups) - 1)
    multiply_due(planes)
    total = norm_ref[...]
    for k in range(2 * planes):
        block = solved[k]
        total = total + jnp.sum(block * block, axis=0, keepdims=True)
    norm_out[...] = total

    for index, (slot, p, target) in enumerate(pending):
        panel_copy(panel.at[slot, span(p)], slot, p, index, target).wait_send()
    for j in range(planes):
        @pl.when(z >= j)
        def _():
            lower_copy(j).wait_send()
    for k in range(planes):
        dist = (z - k + planes) % planes
        for half in range(2):
            @pl.when(dist <= (3 if k < last else 0))
            def _():
                solved_copy(k, half, to_z_next, 0).wait_send()

            if k == last:
                @pl.when(dist == 0)
                def _():
                    direct_copy(half).wait_send()

            @pl.when((dist == 0) | (dist >= 6) | ((dist == 3) | (dist == 4) if k == last else dist == 0))
            def _():
                solved_copy(k, half, to_z_prev, 1).wait_send()


def shards(diag_block, z_panel, panel_below, z_trail, norm_sq):
    height = panel_below.shape[0]
    dma = pltpu.SemaphoreType.DMA
    norm_out, update = pl.pallas_call(
        kernel,
        out_shape=(
            jax.ShapeDtypeStruct((1, T), F32),
            jax.ShapeDtypeStruct((height, T), F32),
        ),
        in_specs=[pl.BlockSpec(memory_space=pl.ANY)] * 3 + [pl.BlockSpec(memory_space=pltpu.VMEM)],
        out_specs=(pl.BlockSpec(memory_space=pltpu.VMEM),) * 2,
        scratch_shapes=[
            pltpu.VMEM((16, height, T), F32),
            pltpu.VMEM((2, 8, T, 2 * T), F32),
            pltpu.VMEM((2, T, T), F32),
            pltpu.VMEM((2 * T, T), F32),
            pltpu.VMEM((16, T, T), F32),
            pltpu.VMEM((16, 2 * T, 2 * T), BF16),
            pltpu.VMEM((3, T, 2 * T), BF16),
            dma((10,)), dma((64,)), dma((16, PIECES)), dma((8,)), dma((8,)),
            dma((1,)), dma((1,)), dma((2, 16)), dma((16,)), dma((2,)),
        ],
        compiler_params=pltpu.CompilerParams(
            collective_id=0, has_side_effects=True, vmem_limit_bytes=67_043_328
        ),
        name="panel_update",
    )(diag_block, z_panel, panel_below, norm_sq.reshape(1, T))
    return norm_out.reshape(T), z_trail - update


def solution(mesh):
    return jax.shard_map(
        shards,
        mesh=mesh,
        in_specs=(P("row", None), P("row", "col"), P("row", "col"), P("row", "col"), P("col")),
        out_specs=(P("col"), P("row", "col")),
        check_vma=False,
    )
```
